32 devices in a mesh: fsdp: 8 (over y, x, core), rep: 4 (over z).
Axes of the slice: x: 2, y: 2, z: 4, core: 2. Of those that a mesh axis runs over, the one named last changes fastest.
Arguments:
- pseudo_grads: float32 [4, 96, 8192], P('rep', 'fsdp'), may hold values from -6 to 6
- counts: int32 [4], P('rep'), may hold values from 4000 to 10999, as said below
- master: float32 [96, 8192], P('fsdp'), may hold values from -6 to 6
- momentum: float32 [96, 8192], P('fsdp'), may hold values from -2 to 2
Outputs:
- new_fragment: bfloat16 [96, 8192], P('fsdp')
- new_master: float32 [96, 8192], P('fsdp')
- new_momentum: float32 [96, 8192], P('fsdp')
The draws below stay inside these ranges and needn't reach their ends.
Inputs may be any that keep to these rules, and one draw needn't show every extreme that they name: kept-token counts of the replica groups, positive.
All inputs are finite; a program needn't handle non-finite values.
Results may differ from the reference program's by a relative error of at most 0.0004.
Values may be sent and summed in bfloat16 or wider, within the bound.
A program may use at most 64 MiB of HBM per device.

```python
import jax
import jax.numpy as jnp
from jax import lax

D = 8192
ROWS = 96
N_REP = 4


def draw_counts(key, part):
    steps = jnp.arange(N_REP, dtype=jnp.int32)
    jitter = jax.random.randint(jax.random.fold_in(key, 17), (N_REP,), 0, 1000, dtype=jnp.int32)
    jitter = jitter.at[0].set(0).at[N_REP - 1].set(999)
    return (1000 * (N_REP + 2 * steps) + jitter).astype(jnp.int32)


def block_scale(key, shape, split, least, top_value):
    factor_of = 1.0
    for axis_at, shards_of in split:
        heights = jax.random.uniform(jax.random.fold_in(jax.random.fold_in(key, 6), axis_at), (shards_of,), jnp.float32, least / len(split), top_value / len(split))
        factor_of = factor_of * jnp.repeat(jnp.exp(heights), shape[axis_at] // shards_of).reshape((-1,) + (1,) * (len(shape) - 1 - axis_at))
    return factor_of


def normal_values(rng, extent, scale, reach, cuts=(), kind=jnp.bfloat16):
    drawn = jax.random.normal(rng, extent, jnp.float32) * scale
    if len(cuts) > 0:
        drawn = block_scale(rng, extent, cuts, -0.22, 0.18) * drawn
    return jnp.clip(drawn, min=-reach, max=reach).astype(kind)


def setup_inputs(seed: int = 0) -> dict:
    key_list = jax.random.split(jax.random.key(seed), 5)
    pseudo_grads = normal_values(key_list[0], (N_REP, ROWS, D), 1.0, 6.0, ((0, 4), (1, 8)), jnp.float32)
    counts = draw_counts(jax.random.fold_in(key_list[4], 71), 0)
    master = normal_values(key_list[2], (ROWS, D), 1.0, 6.0, ((0, 8),), jnp.float32)
    momentum = normal_values(key_list[3], (ROWS, D), 0.3, 2.0, ((0, 8),), jnp.float32)
    return {"pseudo_grads": pseudo_grads, "counts": counts, "master": master, "momentum": momentum}


outer_momentum = 0.9
outer_rate = 0.7


def reference(pseudo_grads, counts, master, momentum):
    weights = counts.astype(jnp.float32)
    all_tokens = jnp.sum(weights)
    summed = jnp.einsum("g,grd->rd", weights, pseudo_grads, precision=lax.Precision.HIGHEST)
    outer_grad = summed / all_tokens
    new_momentum = outer_momentum * momentum + outer_grad
    new_master = master - outer_rate * (outer_grad + outer_momentum * new_momentum)
    return new_master.astype(jnp.bfloat16), new_master, new_momentum
```

```python
import functools

import jax
import jax.numpy as jnp
from jax import lax
from jax.experimental import pallas as pl
from jax.experimental.pallas import tpu as pltpu
from jax.sharding import PartitionSpec as P

outer_momentum = 0.9
outer_rate = 0.7

LANES = 128
CHUNKS = 8
LAG = 3
TOP = 32767.0
TINY = 1e-30
MESH = pl.DeviceIdType.MESH


def pieces(width):
    return [slice(k * LANES, (k + 1) * LANES) for k in range(width // LANES)]


def encode(parts):
    top = jnp.abs(parts[0])
    for part in parts[1:]:
        top = jnp.maximum(top, jnp.abs(part))
    top = jnp.maximum(jnp.max(top, axis=0, keepdims=True), TINY)
    inverse = TOP / top
    return [jnp.round(part * inverse) for part in parts], top * (1.0 / TOP)


def kernel(
    n, chunks, counts_ref, grads_ref, out_ref,
    own, inward, inward_meta, half, half_meta, total, total_meta,
    load_sem, send_a, send_b, recv_in, recv_half, recv_total,
):
    me = lax.axis_index("rep")
    middle = n // 2
    side = (me >= middle).astype(jnp.int32)
    step_in = 1 - 2 * side
    near, far = me + step_in, me - step_in
    is_middle = (me == middle - 1) | (me == middle)
    has_far = (me > 0) & (me < n - 1)
    width = own.shape[2]
    columns = pieces(width)

    def load(c):
        return pltpu.make_async_copy(
            grads_ref.at[0, :, pl.ds(c * width, width)], own.at[c], load_sem.at[c]
        )

    def remote(src, dst, send, recv, device):
        return pltpu.make_async_remote_copy(
            src_ref=src, dst_ref=dst, send_sem=send, recv_sem=recv,
            device_id={"rep": device}, device_id_type=MESH,
        )

    def to_near(c):
        return (
            remote(half.at[side, c], inward.at[c], send_a.at[c, 0], recv_in.at[c, 0], near),
            remote(half_meta.at[side, c], inward_meta.at[c], send_a.at[c, 1], recv_in.at[c, 1], near),
        )

    def across(c):
        return (
            remote(half.at[side, c], half.at[side, c], send_a.at[c, 0], recv_half.at[c, 0], near),
            remote(half_meta.at[side, c], half_meta.at[side, c], send_a.at[c, 1], recv_half.at[c, 1], near),
        )

    def arriving_half(c):
        return (
            remote(half.at[1 - side, c], half.at[1 - side, c], send_a.at[c, 0], recv_half.at[c, 0], near),
            remote(half_meta.at[1 - side, c], half_meta.at[1 - side, c], send_a.at[c, 1], recv_half.at[c, 1], near),
        )

    def to_far(c):
        return (
            remote(total.at[c], total.at[c], send_b.at[c, 0], recv_total.at[c, 0], far),
            remote(total_meta.at[c], total_meta.at[c], send_b.at[c, 1], recv_total.at[c, 1], far),
        )

    def start(copies):
        for copy in copies:
            copy.start()

    def wait_recv(copies):
        for copy in copies:
            copy.wait_recv()

    def wait_send(copies):
        for copy in copies:
            copy.wait_send()

    for c in range(chunks):
        load(c).start()

    barrier = pltpu.get_barrier_semaphore()

    @pl.when(me > 0)
    def _():
        pl.semaphore_signal(barrier, inc=1, device_id={"rep": me - 1}, device_id_type=MESH)

    @pl.when(me < n - 1)
    def _():
        pl.semaphore_signal(barrier, inc=1, device_id={"rep": me + 1}, device_id_type=MESH)

    tokens = jnp.full((1, LANES), counts_ref[0], jnp.int32).astype(jnp.float32)

    def keep_partial(c, parts, held):
        codes, step = encode(parts)
        for at, code in zip(columns, codes):
            half[side, c, :, at] = code.astype(jnp.int16)
        half_meta[side, c, 0:1, :] = step
        half_meta[side, c, 1:2, :] = held

    def own_partial(c):
        load(c).wait()
        keep_partial(c, [own[c, :, at] for at in columns], tokens)

    def joined_partial(c):
        load(c).wait()
        wait_recv(to_near(c))
        there = inward_meta[c, 1:2, :]
        held = there + tokens
        share, mine = there * inward_meta[c, 0:1, :] / held, tokens / held
        keep_partial(
            c,
            [inward[c, :, at].astype(jnp.float32) * share + own[c, :, at] * mine for at in columns],
            held,
        )

    def middle_total(c):
        wait_recv(arriving_half(c))
        low, high = half_meta[0, c, 1:2, :], half_meta[1, c, 1:2, :]
        all_tokens = low + high
        low_share = low * half_meta[0, c, 0:1, :] / all_tokens
        high_share = high * half_meta[1, c, 0:1, :] / all_tokens
        codes, step = encode(
            [
                half[0, c, :, at].astype(jnp.float32) * low_share
                + half[1, c, :, at].astype(jnp.float32) * high_share
                for at in columns
            ]
        )
        for at, code in zip(columns, codes):
            total[c, :, at] = code.astype(jnp.int16)
        total_meta[c, 0:1, :] = step

        @pl.when(has_far)
        def _():
            start(to_far(c))

        for k, code in enumerate(codes):
            out_ref[:, c * width + k * LANES : c * width + (k + 1) * LANES] = code * step

    def outer_total(c):
        wait_recv(to_far(c))

        @pl.when(has_far)
        def _():
            start(to_far(c))

        step = total_meta[c, 0:1, :]
        for k, at in enumerate(columns):
            out_ref[:, c * width + k * LANES : c * width + (k + 1) * LANES] = (
                total[c, :, at].astype(jnp.float32) * step
            )

    half_meta[side] = jnp.zeros(half_meta.shape[1:], jnp.float32)
    total_meta[...] = jnp.zeros(total_meta.shape, jnp.float32)

    pl.semaphore_wait(barrier, (me > 0).astype(jnp.int32) + (me < n - 1).astype(jnp.int32))

    if n > 3:
        @pl.when(is_middle)
        def _():
            for t in range(chunks + LAG):
                if t < chunks:
                    joined_partial(t)
                    start(across(t))
                if t >= LAG:
                    middle_total(t - LAG)

        @pl.when(jnp.logical_not(is_middle))
        def _():
            for c in range(chunks):
                @pl.when(has_far)
                def _():
                    joined_partial(c)

                @pl.when(jnp.logical_not(has_far))
                def _():
                    own_partial(c)

                start(to_near(c))
            for c in range(chunks):
                outer_total(c)
    else:
        for c in range(chunks):
            own_partial(c)
            start(across(c))
        for c in range(chunks):
            middle_total(c)

    for c in range(chunks):
        wait_send(to_near(c))

    @pl.when(has_far)
    def _():
        for c in range(chunks):
            wait_send(to_far(c))


def weighted_mean(n, counts, pseudo_grads):
    rows, depth = pseudo_grads.shape[1:]
    chunks = CHUNKS
    while depth % (chunks * LANES):
        chunks //= 2
    width = depth // chunks
    codes = functools.partial(pltpu.VMEM, dtype=jnp.int16)
    metas = functools.partial(pltpu.VMEM, dtype=jnp.float32)
    pairs = pltpu.SemaphoreType.DMA((chunks, 2))
    return pl.pallas_call(
        functools.partial(kernel, n, chunks),
        out_shape=jax.ShapeDtypeStruct((rows, depth), jnp.float32),
        in_specs=[
            pl.BlockSpec(memory_space=pltpu.SMEM),
            pl.BlockSpec(memory_space=pl.ANY),
        ],
        out_specs=pl.BlockSpec(memory_space=pltpu.VMEM),
        scratch_shapes=[
            pltpu.VMEM((chunks, rows, width), jnp.float32),
            codes((chunks, rows, width)),
            metas((chunks, 8, LANES)),
            codes((2, chunks, rows, width)),
            metas((2, chunks, 8, LANES)),
            codes((chunks, rows, width)),
            metas((chunks, 8, LANES)),
            pltpu.SemaphoreType.DMA((chunks,)),
            pairs, pairs, pairs, pairs, pairs,
        ],
        compiler_params=pltpu.CompilerParams(collective_id=0, has_side_effects=True),
    )(counts, pseudo_grads)


def solution(mesh):
    n = mesh.shape["rep"]

    def shards(pseudo_grads, counts, master, momentum):
        outer_grad = weighted_mean(n, counts, pseudo_grads) if n > 1 else pseudo_grads[0]
        new_momentum = outer_momentum * momentum + outer_grad
        new_master = master - outer_rate * (outer_grad + outer_momentum * new_momentum)
        new_fragment = new_master.astype(jnp.bfloat16)
        return (new_fragment, new_master, new_momentum)

    placed = (P("rep", "fsdp", None), P("rep"), P("fsdp", None), P("fsdp", None))
    return jax.shard_map(
        shards,
        mesh=mesh,
        in_specs=placed,
        out_specs=(P("fsdp", None), P("fsdp", None), P("fsdp", None)),
        check_vma=False,
    )
```

```python
import functools

import jax
import jax.numpy as jnp
from jax import lax
from jax.experimental import pallas as pl
from jax.experimental.pallas import tpu as pltpu
from jax.sharding import PartitionSpec as P

outer_momentum = 0.9
outer_rate = 0.7

LANES = 128
SUBLANES = 8
CHUNKS = 4
LAG = 2
TOP = 32767.0
TINY = 1e-30
MESH = pl.DeviceIdType.MESH


def encode(parts):
    top = jnp.abs(parts[0])
    for part in parts[1:]:
        top = jnp.maximum(top, jnp.abs(part))
    top = jnp.maximum(jnp.max(top, axis=0, keepdims=True), TINY)
    inverse = TOP / top
    return [jnp.round(part * inverse) for part in parts], top * (1.0 / TOP)


def kernel(
    n, chunks, counts_ref, grads_ref, out_ref,
    own, inward, inward_meta, half, half_meta, total, total_meta,
    load_sem, send_a, send_b, recv_in, recv_half, recv_total,
):
    me = lax.axis_index("rep")
    middle = n // 2
    side = (me >= middle).astype(jnp.int32)
    step_in = 1 - 2 * side
    near, far = me + step_in, me - step_in
    is_middle = (me == middle - 1) | (me == middle)
    has_far = (me > 0) & (me < n - 1)
    rows, tiles = own.shape[0], own.shape[1] // chunks
    blocks = [(r, t) for r in range(rows) for t in range(0, tiles, SUBLANES)]

    def put(ref, codes):
        for k in range(0, len(codes), 2):
            pair = jnp.concatenate(codes[k : k + 2], axis=0)
            ref[k // 2, : pair.shape[0]] = pair.astype(jnp.int16)

    def get(ref):
        for k in range(0, len(blocks), 2):
            pair = ref[k // 2].astype(jnp.float32)
            yield pair[:SUBLANES]
            if k + 1 < len(blocks):
                yield pair[SUBLANES:]

    def own_parts(c):
        return [own[r, c * tiles + t : c * tiles + t + SUBLANES] for r, t in blocks]

    def put_out(c, parts):
        for (r, t), part in zip(blocks, parts):
            at = c * tiles + t
            out_ref[r // SUBLANES, at : at + SUBLANES, r % SUBLANES] = part

    def load(c):
        return pltpu.make_async_copy(
            grads_ref.at[:, pl.ds(c * tiles, tiles)], own.at[:, pl.ds(c * tiles, tiles)], load_sem.at[c]
        )

    def remote(src, dst, send, recv, device):
        return pltpu.make_async_remote_copy(
            src_ref=src, dst_ref=dst, send_sem=send, recv_sem=recv,
            device_id={"rep": device}, device_id_type=MESH,
        )

    def to_near(c):
        return (
            remote(half.at[side, c], inward.at[c], send_a.at[c, 0], recv_in.at[c, 0], near),
            remote(half_meta.at[side, c], inward_meta.at[c], send_a.at[c, 1], recv_in.at[c, 1], near),
        )

    def across(c):
        return (
            remote(half.at[side, c], half.at[side, c], send_a.at[c, 0], recv_half.at[c, 0], near),
            remote(half_meta.at[side, c], half_meta.at[side, c], send_a.at[c, 1], recv_half.at[c, 1], near),
        )

    def arriving_half(c):
        return (
            remote(half.at[1 - side, c], half.at[1 - side, c], send_a.at[c, 0], recv_half.at[c, 0], near),
            remote(half_meta.at[1 - side, c], half_meta.at[1 - side, c], send_a.at[c, 1], recv_half.at[c, 1], near),
        )

    def to_far(c):
        return (
            remote(total.at[c], total.at[c], send_b.at[c, 0], recv_total.at[c, 0], far),
            remote(total_meta.at[c], total_meta.at[c], send_b.at[c, 1], recv_total.at[c, 1], far),
        )

    def start(copies):
        for copy in copies:
            copy.start()

    def wait_recv(copies):
        for copy in copies:
            copy.wait_recv()

    def wait_send(copies):
        for copy in copies:
            copy.wait_send()

    for c in range(chunks):
        load(c).start()

    barrier = pltpu.get_barrier_semaphore()

    @pl.when(me > 0)
    def _():
        pl.semaphore_signal(barrier, inc=1, device_id={"rep": me - 1}, device_id_type=MESH)

    @pl.when(me < n - 1)
    def _():
        pl.semaphore_signal(barrier, inc=1, device_id={"rep": me + 1}, device_id_type=MESH)

    tokens = jnp.full((1, LANES), counts_ref[0], jnp.int32).astype(jnp.float32)

    def keep_partial(c, parts, held):
        codes, step = encode(parts)
        put(half.at[side, c], codes)
        half_meta[side, c, 0:1, :] = step
        half_meta[side, c, 1:2, :] = held

    def own_partial(c):
        load(c).wait()
        keep_partial(c, own_parts(c), tokens)

    def joined_partial(c):
        load(c).wait()
        wait_recv(to_near(c))
        there = inward_meta[c, 1:2, :]
        held = there + tokens
        share, mine = there * inward_meta[c, 0:1, :] / held, tokens / held
        keep_partial(
            c,
            [there * share + here * mine for there, here in zip(get(inward.at[c]), own_parts(c))],
            held,
        )

    def middle_total(c):
        wait_recv(arriving_half(c))
        low, high = half_meta[0, c, 1:2, :], half_meta[1, c, 1:2, :]
        all_tokens = low + high
        low_share = low * half_meta[0, c, 0:1, :] / all_tokens
        high_share = high * half_meta[1, c, 0:1, :] / all_tokens
        codes, step = encode(
            [
                low_part * low_share + high_part * high_share
                for low_part, high_part in zip(get(half.at[0, c]), get(half.at[1, c]))
            ]
        )
        put(total.at[c], codes)
        total_meta[c, 0:1, :] = step

        @pl.when(has_far)
        def _():
            start(to_far(c))

        put_out(c, [code * step for code in codes])

    def outer_total(c):
        wait_recv(to_far(c))

        @pl.when(has_far)
        def _():
            start(to_far(c))

        step = total_meta[c, 0:1, :]
        put_out(c, [part * step for part in get(total.at[c])])

    half_meta[side] = jnp.zeros(half_meta.shape[1:], jnp.float32)
    total_meta[...] = jnp.zeros(total_meta.shape, jnp.float32)

    pl.semaphore_wait(barrier, (me > 0).astype(jnp.int32) + (me < n - 1).astype(jnp.int32))

    if n > 3:
        @pl.when(is_middle)
        def _():
            for t in range(chunks + LAG):
                if t < chunks:
                    joined_partial(t)
                    start(across(t))
                if t >= LAG:
                    middle_total(t - LAG)

        @pl.when(jnp.logical_not(is_middle))
        def _():
            for c in range(chunks):
                @pl.when(has_far)
                def _():
                    joined_partial(c)

                @pl.when(jnp.logical_not(has_far))
                def _():
                    own_partial(c)

                start(to_near(c))
            for c in range(chunks):
                outer_total(c)
    else:
        for c in range(chunks):
            own_partial(c)
            start(across(c))
        for c in range(chunks):
            middle_total(c)

    for c in range(chunks):
        wait_send(to_near(c))

    @pl.when(has_far)
    def _():
        for c in range(chunks):
            wait_send(to_far(c))


def weighted_mean(n, counts, pseudo_grads):
    rows, depth = pseudo_grads.shape[1:]
    tiles = depth // LANES
    chunks = CHUNKS
    while tiles % (chunks * SUBLANES):
        chunks //= 2
    code = (-(-(rows * tiles // SUBLANES // chunks) // 2), 2 * SUBLANES, LANES)
    meta = (2, LANES)
    groups = -(-rows // SUBLANES)
    pairs = pltpu.SemaphoreType.DMA((chunks, 2))
    out = pl.pallas_call(
        functools.partial(kernel, n, chunks),
        out_shape=jax.ShapeDtypeStruct((groups, tiles, SUBLANES, LANES), jnp.float32),
        in_specs=[
            pl.BlockSpec(memory_space=pltpu.SMEM),
            pl.BlockSpec(memory_space=pl.ANY),
        ],
        out_specs=pl.BlockSpec(memory_space=pltpu.VMEM),
        scratch_shapes=[
            pltpu.VMEM((rows, tiles, LANES), jnp.float32),
            pltpu.VMEM((chunks, *code), jnp.int16),
            pltpu.VMEM((chunks, *meta), jnp.float32),
            pltpu.VMEM((2, chunks, *code), jnp.int16),
            pltpu.VMEM((2, chunks, *meta), jnp.float32),
            pltpu.VMEM((chunks, *code), jnp.int16),
            pltpu.VMEM((chunks, *meta), jnp.float32),
            pltpu.SemaphoreType.DMA((chunks,)),
            pairs, pairs, pairs, pairs, pairs,
        ],
        compiler_params=pltpu.CompilerParams(collective_id=0, has_side_effects=True),
    )(counts, pseudo_grads.reshape(rows, tiles, LANES))
    return out.transpose(0, 2, 1, 3).reshape(groups * SUBLANES, depth)[:rows]


def solution(mesh):
    n = mesh.shape["rep"]

    def shards(pseudo_grads, counts, master, momentum):
        outer_grad = weighted_mean(n, counts, pseudo_grads) if n > 1 else pseudo_grads[0]
        new_momentum = outer_momentum * momentum + outer_grad
        new_master = master - outer_rate * (outer_grad + outer_momentum * new_momentum)
        new_fragment = new_master.astype(jnp.bfloat16)
        return (new_fragment, new_master, new_momentum)

    placed = (P("rep", "fsdp", None), P("rep"), P("fsdp", None), P("fsdp", None))
    return jax.shard_map(
        shards,
        mesh=mesh,
        in_specs=placed,
        out_specs=(P("fsdp", None), P("fsdp", None), P("fsdp", None)),
        check_vma=False,
    )
```

```python
import functools

import jax
import jax.numpy as jnp
from jax import lax
from jax.experimental import pallas as pl
from jax.experimental.pallas import tpu as pltpu
from jax.sharding import PartitionSpec as P

outer_momentum = 0.9
outer_rate = 0.7

LANES = 128
SUBLANES = 8
CHUNKS = 8
LAG = 5
VLIM = 8 * 1024 * 1024
TOP = 32767.0
TINY = 1e-30
MESH = pl.DeviceIdType.MESH


def encode(parts):
    top = jnp.abs(parts[0])
    for part in parts[1:]:
        top = jnp.maximum(top, jnp.abs(part))
    top = jnp.maximum(jnp.max(top, axis=0, keepdims=True), TINY)
    inverse = TOP / top
    return [jnp.round(part * inverse) for part in parts], top * (1.0 / TOP)


def kernel(
    n, chunks, counts_ref, grads_ref, out_ref,
    own, inward, inward_meta, half, half_meta, total, total_meta,
    load_sem, send_a, send_b, recv_in, recv_half, recv_total,
):
    me = lax.axis_index("rep")
    middle = n // 2
    side = (me >= middle).astype(jnp.int32)
    step_in = 1 - 2 * side
    near, far = me + step_in, me - step_in
    is_middle = (me == middle - 1) | (me == middle)
    has_far = (me > 0) & (me < n - 1)
    rows, tiles = own.shape[0], own.shape[1] // chunks
    blocks = [(r, t) for r in range(rows) for t in range(0, tiles, SUBLANES)]

    def put(ref, codes):
        for k in range(0, len(codes), 2):
            pair = jnp.concatenate(codes[k : k + 2], axis=0)
            ref[k // 2, : pair.shape[0]] = pair.astype(jnp.int16)

    def get(ref):
        for k in range(0, len(blocks), 2):
            pair = ref[k // 2].astype(jnp.float32)
            yield pair[:SUBLANES]
            if k + 1 < len(blocks):
                yield pair[SUBLANES:]

    def own_parts(c):
        return [own[r, c * tiles + t : c * tiles + t + SUBLANES] for r, t in blocks]

    def put_out(c, parts):
        for (r, t), part in zip(blocks, parts):
            at = c * tiles + t
            out_ref[r // SUBLANES, at : at + SUBLANES, r % SUBLANES] = part

    def load(c):
        return pltpu.make_async_copy(
            grads_ref.at[:, pl.ds(c * tiles, tiles)], own.at[:, pl.ds(c * tiles, tiles)], load_sem.at[c]
        )

    def remote(src, dst, send, recv, device):
        return pltpu.make_async_remote_copy(
            src_ref=src, dst_ref=dst, send_sem=send, recv_sem=recv,
            device_id={"rep": device}, device_id_type=MESH,
        )

    def to_near(c):
        return (
            remote(half.at[side, c], inward.at[c], send_a.at[c, 0], recv_in.at[c, 0], near),
            remote(half_meta.at[side, c], inward_meta.at[c], send_a.at[c, 1], recv_in.at[c, 1], near),
        )

    def across(c):
        return (
            remote(half.at[side, c], half.at[side, c], send_a.at[c, 0], recv_half.at[c, 0], near),
            remote(half_meta.at[side, c], half_meta.at[side, c], send_a.at[c, 1], recv_half.at[c, 1], near),
        )

    def arriving_half(c):
        return (
            remote(half.at[1 - side, c], half.at[1 - side, c], send_a.at[c, 0], recv_half.at[c, 0], near),
            remote(half_meta.at[1 - side, c], half_meta.at[1 - side, c], send_a.at[c, 1], recv_half.at[c, 1], near),
        )

    def to_far(c):
        return (
            remote(total.at[c], total.at[c], send_b.at[c, 0], recv_total.at[c, 0], far),
            remote(total_meta.at[c], total_meta.at[c], send_b.at[c, 1], recv_total.at[c, 1], far),
        )

    def start(copies):
        for copy in copies:
            copy.start()

    def wait_recv(copies):
        for copy in copies:
            copy.wait_recv()

    def wait_send(copies):
        for copy in copies:
            copy.wait_send()

    for c in range(chunks):
        load(c).start()

    barrier = pltpu.get_barrier_semaphore()

    @pl.when(me > 0)
    def _():
        pl.semaphore_signal(barrier, inc=1, device_id={"rep": me - 1}, device_id_type=MESH)

    @pl.when(me < n - 1)
    def _():
        pl.semaphore_signal(barrier, inc=1, device_id={"rep": me + 1}, device_id_type=MESH)

    tokens = jnp.full((1, LANES), counts_ref[0], jnp.int32).astype(jnp.float32)

    def keep_partial(c, parts, held):
        codes, step = encode(parts)
        put(half.at[side, c], codes)
        half_meta[side, c, 0:1, :] = step
        half_meta[side, c, 1:2, :] = held

    def own_partial(c):
        load(c).wait()
        keep_partial(c, own_parts(c), tokens)

    def joined_partial(c):
        load(c).wait()
        wait_recv(to_near(c))
        there = inward_meta[c, 1:2, :]
        held = there + tokens
        share, mine = there * inward_meta[c, 0:1, :] / held, tokens / held
        keep_partial(
            c,
            [there * share + here * mine for there, here in zip(get(inward.at[c]), own_parts(c))],
            held,
        )

    def middle_total(c):
        wait_recv(arriving_half(c))
        low, high = half_meta[0, c, 1:2, :], half_meta[1, c, 1:2, :]
        all_tokens = low + high
        low_share = low * half_meta[0, c, 0:1, :] / all_tokens
        high_share = high * half_meta[1, c, 0:1, :] / all_tokens
        codes, step = encode(
            [
                low_part * low_share + high_part * high_share
                for low_part, high_part in zip(get(half.at[0, c]), get(half.at[1, c]))
            ]
        )
        put(total.at[c], codes)
        total_meta[c, 0:1, :] = step

        @pl.when(has_far)
        def _():
            start(to_far(c))

        put_out(c, [code * step for code in codes])

    def outer_total(c):
        wait_recv(to_far(c))

        @pl.when(has_far)
        def _():
            start(to_far(c))

        step = total_meta[c, 0:1, :]
        put_out(c, [part * step for part in get(total.at[c])])

    half_meta[side] = jnp.zeros(half_meta.shape[1:], jnp.float32)
    total_meta[...] = jnp.zeros(total_meta.shape, jnp.float32)

    pl.semaphore_wait(barrier, (me > 0).astype(jnp.int32) + (me < n - 1).astype(jnp.int32))

    if n > 3:
        @pl.when(is_middle)
        def _():
            for t in range(chunks + LAG):
                if t < chunks:
                    joined_partial(t)
                    start(across(t))
                if t >= LAG:
                    middle_total(t - LAG)

        @pl.when(jnp.logical_not(is_middle))
        def _():
            for c in range(chunks):
                @pl.when(has_far)
                def _():
                    joined_partial(c)

                @pl.when(jnp.logical_not(has_far))
                def _():
                    own_partial(c)

                start(to_near(c))
            for c in range(chunks):
                outer_total(c)
    else:
        for c in range(chunks):
            own_partial(c)
            start(across(c))
        for c in range(chunks):
            middle_total(c)

    for c in range(chunks):
        wait_send(to_near(c))

    @pl.when(has_far)
    def _():
        for c in range(chunks):
            wait_send(to_far(c))


def weighted_mean(n, counts, pseudo_grads):
    rows, depth = pseudo_grads.shape[1:]
    tiles = depth // LANES
    chunks = CHUNKS
    while tiles % (chunks * SUBLANES):
        chunks //= 2
    code = (-(-(rows * tiles // SUBLANES // chunks) // 2), 2 * SUBLANES, LANES)
    meta = (2, LANES)
    groups = -(-rows // SUBLANES)
    pairs = pltpu.SemaphoreType.DMA((chunks, 2))
    out = pl.pallas_call(
        functools.partial(kernel, n, chunks),
        out_shape=jax.ShapeDtypeStruct((groups, tiles, SUBLANES, LANES), jnp.float32),
        in_specs=[
            pl.BlockSpec(memory_space=pltpu.SMEM),
            pl.BlockSpec(memory_space=pltpu.HBM),
        ],
        out_specs=pl.BlockSpec(memory_space=pltpu.VMEM),
        scratch_shapes=[
            pltpu.VMEM((rows, tiles, LANES), jnp.float32),
            pltpu.VMEM((chunks, *code), jnp.int16),
            pltpu.VMEM((chunks, *meta), jnp.float32),
            pltpu.VMEM((2, chunks, *code), jnp.int16),
            pltpu.VMEM((2, chunks, *meta), jnp.float32),
            pltpu.VMEM((chunks, *code), jnp.int16),
            pltpu.VMEM((chunks, *meta), jnp.float32),
            pltpu.SemaphoreType.DMA((chunks,)),
            pairs, pairs, pairs, pairs, pairs,
        ],
        compiler_params=pltpu.CompilerParams(collective_id=0, has_side_effects=True, vmem_limit_bytes=VLIM),
    )(counts, pltpu.with_memory_space_constraint(pseudo_grads.reshape(rows, tiles, LANES), pltpu.HBM))
    return out.transpose(0, 2, 1, 3).reshape(groups * SUBLANES, depth)[:rows]


def solution(mesh):
    n = mesh.shape["rep"]

    def shards(pseudo_grads, counts, master, momentum):
        outer_grad = weighted_mean(n, counts, pseudo_grads) if n > 1 else pseudo_grads[0]
        new_momentum = outer_momentum * momentum + outer_grad
        new_master = master - outer_rate * (outer_grad + outer_momentum * new_momentum)
        new_fragment = new_master.astype(jnp.bfloat16)
        return (new_fragment, new_master, new_momentum)

    placed = (P("rep", "fsdp", None), P("rep"), P("fsdp", None), P("fsdp", None))
    return jax.shard_map(
        shards,
        mesh=mesh,
        in_specs=placed,
        out_specs=(P("fsdp", None), P("fsdp", None), P("fsdp", None)),
        check_vma=False,
    )
```

```python
import functools

import jax
import jax.numpy as jnp
from jax import lax
from jax.experimental import pallas as pl
from jax.experimental.pallas import tpu as pltpu
from jax.sharding import PartitionSpec as P

outer_momentum = 0.9
outer_rate = 0.7

LANES = 128
SUBLANES = 8
CHUNKS = 8
LAG = 5
PARTS = 4
VLIM = 8 * 1024 * 1024
TOP = 32767.0
TINY = 1e-30
MESH = pl.DeviceIdType.MESH


def encode(parts):
    top = jnp.abs(parts[0])
    for part in parts[1:]:
        top = jnp.maximum(top, jnp.abs(part))
    top = jnp.maximum(jnp.max(top, axis=0, keepdims=True), TINY)
    inverse = TOP / top
    return [jnp.round(part * inverse) for part in parts], top * (1.0 / TOP)


def kernel(
    n, chunks, counts_ref, grads_ref, momentum_ref, out_ref, momentum_out, momentum_sem,
    own, inward, inward_meta, half, half_meta, total, total_meta,
    load_sem, send_a, send_b, recv_in, recv_half, recv_total,
):
    me = lax.axis_index("rep")
    middle = n // 2
    side = (me >= middle).astype(jnp.int32)
    step_in = 1 - 2 * side
    near, far = me + step_in, me - step_in
    is_middle = (me == middle - 1) | (me == middle)
    has_far = (me > 0) & (me < n - 1)
    rows, tiles = own.shape[0], own.shape[1] // chunks
    blocks = [(r, t) for r in range(rows) for t in range(0, tiles, SUBLANES)]

    def put(ref, codes):
        for k in range(0, len(codes), 2):
            pair = jnp.concatenate(codes[k : k + 2], axis=0)
            ref[k // 2, : pair.shape[0]] = pair.astype(jnp.int16)

    def get(ref):
        for k in range(0, len(blocks), 2):
            pair = ref[k // 2].astype(jnp.float32)
            yield pair[:SUBLANES]
            if k + 1 < len(blocks):
                yield pair[SUBLANES:]

    def own_parts(c):
        return [own[r, c * tiles + t : c * tiles + t + SUBLANES] for r, t in blocks]

    def put_out(c, parts):
        for (r, t), part in zip(blocks, parts):
            at = c * tiles + t
            out_ref[r // SUBLANES, at : at + SUBLANES, r % SUBLANES] = part

    def load(c):
        return pltpu.make_async_copy(
            grads_ref.at[:, pl.ds(c * tiles, tiles)], own.at[:, pl.ds(c * tiles, tiles)], load_sem.at[c]
        )

    def remote(src, dst, send, recv, device):
        return pltpu.make_async_remote_copy(
            src_ref=src, dst_ref=dst, send_sem=send, recv_sem=recv,
            device_id={"rep": device}, device_id_type=MESH,
        )

    def to_near(c):
        return (
            remote(half.at[side, c], inward.at[c], send_a.at[c, 0], recv_in.at[c, 0], near),
            remote(half_meta.at[side, c], inward_meta.at[c], send_a.at[c, 1], recv_in.at[c, 1], near),
        )

    def across(c):
        return (
            remote(half.at[side, c], half.at[side, c], send_a.at[c, 0], recv_half.at[c, 0], near),
            remote(half_meta.at[side, c], half_meta.at[side, c], send_a.at[c, 1], recv_half.at[c, 1], near),
        )

    def arriving_half(c):
        return (
            remote(half.at[1 - side, c], half.at[1 - side, c], send_a.at[c, 0], recv_half.at[c, 0], near),
            remote(half_meta.at[1 - side, c], half_meta.at[1 - side, c], send_a.at[c, 1], recv_half.at[c, 1], near),
        )

    def to_far(c):
        return (
            remote(total.at[c], total.at[c], send_b.at[c, 0], recv_total.at[c, 0], far),
            remote(total_meta.at[c], total_meta.at[c], send_b.at[c, 1], recv_total.at[c, 1], far),
        )

    def start(copies):
        for copy in copies:
            copy.start()

    def wait_recv(copies):
        for copy in copies:
            copy.wait_recv()

    def wait_send(copies):
        for copy in copies:
            copy.wait_send()

    for c in range(chunks):
        load(c).start()
    momentum_load = pltpu.make_async_copy(momentum_ref, momentum_out, momentum_sem)
    momentum_load.start()

    barrier = pltpu.get_barrier_semaphore()

    @pl.when(me > 0)
    def _():
        pl.semaphore_signal(barrier, inc=1, device_id={"rep": me - 1}, device_id_type=MESH)

    @pl.when(me < n - 1)
    def _():
        pl.semaphore_signal(barrier, inc=1, device_id={"rep": me + 1}, device_id_type=MESH)

    tokens = jnp.full((1, LANES), counts_ref[0], jnp.int32).astype(jnp.float32)

    def keep_partial(c, parts, held):
        codes, step = encode(parts)
        put(half.at[side, c], codes)
        half_meta[side, c, 0:1, :] = step
        half_meta[side, c, 1:2, :] = held

    def own_partial(c):
        load(c).wait()
        keep_partial(c, own_parts(c), tokens)

    def joined_partial(c):
        load(c).wait()
        wait_recv(to_near(c))
        there = inward_meta[c, 1:2, :]
        held = there + tokens
        share, mine = there * inward_meta[c, 0:1, :] / held, tokens / held
        keep_partial(
            c,
            [there * share + here * mine for there, here in zip(get(inward.at[c]), own_parts(c))],
            held,
        )

    def middle_total(c):
        wait_recv(arriving_half(c))
        low, high = half_meta[0, c, 1:2, :], half_meta[1, c, 1:2, :]
        all_tokens = low + high
        low_share = low * half_meta[0, c, 0:1, :] / all_tokens
        high_share = high * half_meta[1, c, 0:1, :] / all_tokens
        codes, step = encode(
            [
                low_part * low_share + high_part * high_share
                for low_part, high_part in zip(get(half.at[0, c]), get(half.at[1, c]))
            ]
        )
        put(total.at[c], codes)
        total_meta[c, 0:1, :] = step

        @pl.when(has_far)
        def _():
            start(to_far(c))

        put_out(c, [code * step for code in codes])

    def outer_total(c):
        wait_recv(to_far(c))

        @pl.when(has_far)
        def _():
            start(to_far(c))

        step = total_meta[c, 0:1, :]
        put_out(c, [part * step for part in get(total.at[c])])

    half_meta[side] = jnp.zeros(half_meta.shape[1:], jnp.float32)
    total_meta[...] = jnp.zeros(total_meta.shape, jnp.float32)

    pl.semaphore_wait(barrier, (me > 0).astype(jnp.int32) + (me < n - 1).astype(jnp.int32))

    if n > 3:
        @pl.when(is_middle)
        def _():
            for t in range(chunks + LAG):
                if t < chunks:
                    joined_partial(t)
                    start(across(t))
                if t >= LAG:
                    middle_total(t - LAG)

        @pl.when(jnp.logical_not(is_middle))
        def _():
            for c in range(chunks):
                @pl.when(has_far)
                def _():
                    joined_partial(c)

                @pl.when(jnp.logical_not(has_far))
                def _():
                    own_partial(c)

                start(to_near(c))
            for c in range(chunks):
                outer_total(c)
    else:
        for c in range(chunks):
            own_partial(c)
            start(across(c))
        for c in range(chunks):
            middle_total(c)

    momentum_load.wait()
    for c in range(chunks):
        wait_send(to_near(c))

    @pl.when(has_far)
    def _():
        for c in range(chunks):
            wait_send(to_far(c))


def weighted_mean(n, counts, pseudo_grads, momentum):
    rows, depth = pseudo_grads.shape[1:]
    tiles = depth // LANES
    chunks = CHUNKS
    while tiles % (chunks * SUBLANES):
        chunks //= 2
    code = (-(-(rows * tiles // SUBLANES // chunks) // 2), 2 * SUBLANES, LANES)
    meta = (2, LANES)
    groups = -(-rows // SUBLANES)
    pairs = pltpu.SemaphoreType.DMA((chunks, 2))
    return pl.pallas_call(
        functools.partial(kernel, n, chunks),
        out_shape=(
            jax.ShapeDtypeStruct((groups, tiles, SUBLANES, LANES), jnp.float32),
            jax.ShapeDtypeStruct((rows, depth), jnp.float32),
        ),
        in_specs=[
            pl.BlockSpec(memory_space=pltpu.SMEM),
            pl.BlockSpec(memory_space=pltpu.HBM),
            pl.BlockSpec(memory_space=pltpu.HBM),
        ],
        out_specs=(pl.BlockSpec(memory_space=pltpu.VMEM),) * 2,
        scratch_shapes=[
            pltpu.SemaphoreType.DMA,
            pltpu.VMEM((rows, tiles, LANES), jnp.float32),
            pltpu.VMEM((chunks, *code), jnp.int16),
            pltpu.VMEM((chunks, *meta), jnp.float32),
            pltpu.VMEM((2, chunks, *code), jnp.int16),
            pltpu.VMEM((2, chunks, *meta), jnp.float32),
            pltpu.VMEM((chunks, *code), jnp.int16),
            pltpu.VMEM((chunks, *meta), jnp.float32),
            pltpu.SemaphoreType.DMA((chunks,)),
            pairs, pairs, pairs, pairs, pairs,
        ],
        compiler_params=pltpu.CompilerParams(collective_id=0, has_side_effects=True, vmem_limit_bytes=VLIM),
    )(
        counts,
        pltpu.with_memory_space_constraint(pseudo_grads.reshape(rows, tiles, LANES), pltpu.HBM),
        pltpu.with_memory_space_constraint(momentum, pltpu.HBM),
    )


def update_kernel(
    grad_ref, master_ref, momentum_ref, fragment_ref, new_master_ref, new_momentum_ref,
    fragment, new_master, new_momentum, sems,
):
    rows, depth = master_ref.shape
    parts = sems.shape[1]
    tiles = depth // LANES // parts
    copies = []
    for c in range(parts):
        for low in range(0, rows, SUBLANES):
            high = min(low + SUBLANES, rows)
            for k in range(c * tiles, (c + 1) * tiles):
                at = (slice(low, high), slice(k * LANES, (k + 1) * LANES))
                outer_grad = grad_ref[low // SUBLANES, k, : high - low]
                moved = outer_momentum * momentum_ref[at] + outer_grad
                stepped = master_ref[at] - outer_rate * (outer_grad + outer_momentum * moved)
                new_momentum[at] = moved
                new_master[at] = stepped
                fragment[at] = stepped.astype(jnp.bfloat16)
        columns = pl.ds(c * tiles * LANES, tiles * LANES)
        for k, (src, dst) in enumerate(
            ((new_momentum, new_momentum_ref), (new_master, new_master_ref), (fragment, fragment_ref))
        ):
            copy = pltpu.make_async_copy(src.at[:, columns], dst.at[:, columns], sems.at[k, c])
            copy.start()
            copies.append(copy)
    for copy in copies:
        copy.wait()


def update(outer_grad, master, momentum):
    rows, depth = master.shape
    parts = PARTS
    while depth // LANES % parts:
        parts //= 2
    shapes = tuple(((rows, depth), kind) for kind in (jnp.bfloat16, jnp.float32, jnp.float32))
    return pl.pallas_call(
        update_kernel,
        out_shape=tuple(jax.ShapeDtypeStruct(*shape) for shape in shapes),
        in_specs=[pl.BlockSpec(memory_space=pltpu.VMEM)] * 3,
        out_specs=(pl.BlockSpec(memory_space=pltpu.HBM),) * 3,
        scratch_shapes=[
            *(pltpu.VMEM(*shape) for shape in shapes),
            pltpu.SemaphoreType.DMA((3, parts)),
        ],
        compiler_params=pltpu.CompilerParams(vmem_limit_bytes=VLIM),
    )(outer_grad, master, momentum)


def solution(mesh):
    n = mesh.shape["rep"]

    def shards(pseudo_grads, counts, master, momentum):
        if n > 1:
            outer_grad, momentum = weighted_mean(n, counts, pseudo_grads, momentum)
            return update(outer_grad, master, momentum)
        outer_grad = pseudo_grads[0]
        new_momentum = outer_momentum * momentum + outer_grad
        new_master = master - outer_rate * (outer_grad + outer_momentum * new_momentum)
        return (new_master.astype(jnp.bfloat16), new_master, new_momentum)

    placed = (P("rep", "fsdp", None), P("rep"), P("fsdp", None), P("fsdp", None))
    return jax.shard_map(
        shards,
        mesh=mesh,
        in_specs=placed,
        out_specs=(P("fsdp", None), P("fsdp", None), P("fsdp", None)),
        check_vma=False,
    )
```
